32 devices in a mesh: parts: 2 (over y), expert: 16 (over z, x, core), dp: 1.
Axes of the slice: x: 2, y: 2, z: 4, core: 2. Of those that a mesh axis runs over, the one named last changes fastest.
Arguments:
- tokens: bfloat16 [2048, 2048], P(('parts', 'expert', 'dp')), parts along dimension 0, may hold values from -6 to 6
- expert_ids: int32 [2048, 8], P(('parts', 'expert', 'dp')), parts along dimension 0, may hold values from 0 to 15, all different within a row; in each aligned block of 64 rows (0 to 63, 64 to 127, ...) at most 64 rows name the same one
- router_weights: float32 [2048, 8], P(('parts', 'expert', 'dp')), parts along dimension 0, may hold values from 0.1 to 1
- w_gate: bfloat16 [16, 2048, 768], P('expert', None, 'dp'), may hold values from -0.125 to 0.125
- w_up: bfloat16 [16, 2048, 768], P('expert', None, 'dp'), may hold values from -0.125 to 0.125
- w_down: bfloat16 [16, 2048, 768], P('expert', None, 'dp'), may hold values from -0.21875 to 0.21875
Outputs:
- mixed: bfloat16 [2048, 2048], P(('parts', 'expert', 'dp')), parts along dimension 0
The draws below stay inside these ranges and needn't reach their ends.
There are 2 independent parts, one for each index of `parts`. The reference program is written for one: setup_inputs(seed, part) draws one part's arguments, and reference() takes and returns one part's arrays. A program takes and returns all parts, laid end to end along the dimension named above; an argument that names none is the same for every part. Nothing has to cross between parts.
Inputs may be any that keep to these rules, and one draw needn't show every extreme that they name: `expert_ids`: each token names 8 different experts. Among the 64 tokens of one device no expert is named more than 64 times, and in every draw some expert is named exactly 64 times by the tokens of some device.
All inputs are finite; a program needn't handle non-finite values.
Results may differ from the reference program's by a relative error of at most 0.008.
Values may be sent and summed in bfloat16 or wider, within the bound.
A program may use at most 128 MiB of HBM per device.

```python
import math
import jax
import jax.numpy as jnp
import numpy as np
from jax import lax

D = 2048
FF = 768
TOP = 8
TOK_DEV = 64
EXPERTS = 16
TOKENS = 1024
CAP = 64
N_EXPERT = 16
N_DP = 1


def block_scale(key, dims, shards, low, high):
    factor_of, own = 1.0, jax.random.fold_in(key, 6)
    for position, shards_of in shards:
        draws = jnp.exp(jax.random.uniform(jax.random.fold_in(own, position), (shards_of,), jnp.float32, low / len(shards), high / len(shards)))
        factor_of = factor_of * jnp.repeat(draws, dims[position] // shards_of).reshape([-1 if axis == position else 1 for axis in range(len(dims))])
    return factor_of


def deal_out(rng, own, number, rows, number_of, top, limit, skew):
    order = jax.random.permutation(rng, number_of)
    packed, ordinary = portions_of(number_of, rows * top, limit, skew, True), portions_of(number_of, rows * top, limit, skew, False)
    places = jnp.arange(number_of)

    def named(sizes, turn):
        used = int((sizes > 0).sum())
        fixed = max(1, used // 4)
        shifted = fixed + (places - fixed + turn * (used - fixed)) % max(1, number_of - fixed)
        return jnp.zeros((number_of,), jnp.int32).at[order[jnp.where(places < fixed, places, shifted)]].set(jnp.asarray(sizes, jnp.int32))

    sizes = jnp.where(number % 4 == 0, named(packed, number // 4), named(ordinary, number - number // 4 - 1))
    mixed = jax.random.permutation(jax.random.fold_in(own, 3), number_of)
    source_of, sink = mixed[0:number_of // 2 * 2:2], mixed[1:number_of // 2 * 2:2]
    room = jnp.minimum(sizes[source_of] - 1, limit - sizes[sink]) // 2
    room = jnp.where((source_of == order[0]) | (sink == order[0]) | (sizes[sink] == 0), 0, jnp.maximum(room, 0))
    shifted = jax.random.randint(jax.random.fold_in(own, 4), (number_of // 2,), 0, 1 << 20) % (room + 1)
    sizes = sizes.at[source_of].add(-shifted).at[sink].add(shifted)
    items = jnp.searchsorted(jnp.cumsum(sizes), jnp.arange(rows * top), side="right").astype(jnp.int32)
    grid = items.reshape(top, rows).T
    grid = grid[jax.random.permutation(jax.random.fold_in(own, 1), rows)]
    turn = jax.random.randint(jax.random.fold_in(own, 2), (rows, 1), 0, top)
    return jnp.take_along_axis(grid, (jnp.arange(top)[None, :] + turn) % top, axis=1)


def portions_of(number_of, total, bound, slope, full):
    portions = [(1 << 20) // math.isqrt(rank ** slope) + 1 for rank in range(1, number_of + 1)]
    largest = bound if full else min(bound, max(-(-total // number_of), total * portions[0] // sum(portions)))
    least = 1 if total - largest >= number_of - 1 else 0
    counts, surplus = [largest] + [least] * (number_of - 1), total - largest - least * (number_of - 1)
    while surplus > 0:
        free = [i for i in range(1, number_of) if counts[i] < largest] or [i for i in range(1, number_of) if counts[i] < bound]
        mass, remaining = sum([portions[i] for i in free]), surplus
        for i in free:
            more = min(bound - counts[i], max(1, remaining * portions[i] // mass), surplus)
            counts[i] = counts[i] + more
            surplus = surplus - more
    return np.array(counts)


def noise(stream_key, shape, scale, reach, cuts=(), kind=jnp.bfloat16):
    gain = block_scale(stream_key, shape, cuts, -0.22, 0.18) if cuts else 1.0
    values = jax.random.normal(stream_key, shape, jnp.float32) * scale * gain
    return jnp.minimum(jnp.maximum(values, -reach), reach).astype(kind)


def setup_inputs(seed: int = 0, part: int = 0) -> dict:
    streams_of = jax.random.split(jax.random.key(seed), 7)
    own_keys = jax.random.split(jax.random.fold_in(streams_of[6], part), 7)
    tokens = noise(own_keys[0], (TOKENS, D), 1.0, 6.0, ((0, 16),))
    expert_ids_keys = jax.random.split(jax.random.fold_in(own_keys[1], 1), TOKENS // TOK_DEV)
    expert_ids_turns = jax.random.permutation(jax.random.fold_in(own_keys[1], 3), TOKENS // TOK_DEV)
    expert_ids = jax.vmap(lambda own, number: deal_out(jax.random.fold_in(own_keys[1], 2), own, number, TOK_DEV, EXPERTS, TOP, CAP, 2))(expert_ids_keys, expert_ids_turns).reshape((TOKENS, TOP))
    router_weights = jnp.clip(jnp.exp(math.log(1.0) - 2.3025851 * jax.random.uniform(own_keys[2], (TOKENS, TOP), jnp.float32) ** block_scale(own_keys[2], (TOKENS, TOP), ((0, 16),), -0.2, 0.2)), 0.1, 1.0)
    w_gate = noise(streams_of[3], (EXPERTS, D, FF), D ** -0.5, 0.125, ((0, 16),))
    w_up = noise(streams_of[4], (EXPERTS, D, FF), D ** -0.5, 0.125, ((0, 16),))
    w_down = noise(streams_of[5], (EXPERTS, D, FF), FF ** -0.5, 0.21875, ((0, 16),))
    return {"tokens": tokens, "expert_ids": expert_ids, "router_weights": router_weights, "w_gate": w_gate, "w_up": w_up, "w_down": w_down}


def reference(tokens, expert_ids, router_weights, w_gate, w_up, w_down):
    maxrows = CAP * N_EXPERT * N_DP
    block = math.gcd(maxrows, 128)
    padded = jnp.concatenate([tokens, jnp.zeros((1, D), jnp.bfloat16)], 0)

    def step(accum, inputs):
        expert, gate_w, up_w, down_w = inputs
        chosen = expert_ids == expert
        weight = jnp.sum(jnp.where(chosen, router_weights, jnp.zeros_like(router_weights)), 1)
        member = jnp.any(chosen, 1)
        count = jnp.sum(member.astype(jnp.int32))
        where_rows = jnp.nonzero(member, size=maxrows, fill_value=TOKENS)[0].astype(jnp.int32)
        rows = padded[where_rows]

        def run(block_rows):
            gate_val = jnp.dot(block_rows, gate_w, preferred_element_type=jnp.float32)
            up_val = jnp.dot(block_rows, up_w, preferred_element_type=jnp.float32)
            hidden = (jax.nn.silu(gate_val) * up_val).astype(jnp.bfloat16)
            return jnp.dot(hidden, down_w.T, preferred_element_type=jnp.float32)

        def empty(block_rows):
            return jnp.zeros((block_rows.shape[0], D), jnp.float32)

        pieces = []
        for index in range(maxrows // block):
            block_rows = rows[index * block:(index + 1) * block]
            pieces.append(lax.cond(index * block < count, run, empty, block_rows))
        expert_out = lax.optimization_barrier(jnp.concatenate(pieces, 0).astype(jnp.bfloat16))
        weights_pad = jnp.concatenate([weight, jnp.zeros((1,), weight.dtype)], 0)[where_rows]
        accum = accum.at[where_rows].add(weights_pad[:, None] * expert_out.astype(jnp.float32))
        return accum, None

    start = jnp.zeros((TOKENS + 1, D), jnp.float32)
    total, unused = lax.scan(step, start, (jnp.arange(EXPERTS, dtype=jnp.int32), w_gate, w_up, w_down))
    return total[:TOKENS].astype(jnp.bfloat16)
```

```python
import math

import jax
import jax.numpy as jnp
from jax import lax
from jax.sharding import PartitionSpec as P


def expert_rows(rows, gate_w, up_w, down_w):
    total = rows.shape[0]
    block = math.gcd(total, 128)
    pieces = []
    for index in range(total // block):
        block_rows = rows[index * block : (index + 1) * block]
        gate_val = jnp.dot(block_rows, gate_w, preferred_element_type=jnp.float32)
        up_val = jnp.dot(block_rows, up_w, preferred_element_type=jnp.float32)
        hidden = (jax.nn.silu(gate_val) * up_val).astype(jnp.bfloat16)
        pieces.append(
            lax.dot_general(
                hidden, down_w, (((1,), (1,)), ((), ())), preferred_element_type=jnp.float32
            )
        )
    return jnp.concatenate(pieces, 0)


def routed_body(cap, tokens, expert_ids, router_weights, w_gate, w_up, w_down):
    tok_count, top = expert_ids.shape
    width = tokens.shape[1]
    experts = lax.axis_size("expert")
    slots_all = experts * cap
    flat_ids = expert_ids.reshape(-1)
    onehot = (flat_ids[:, None] == jnp.arange(experts, dtype=jnp.int32)[None, :]).astype(jnp.int32)
    before = jnp.cumsum(onehot, 0) - onehot
    position = jnp.sum(before * onehot, 1)
    slot = flat_ids * cap + position
    send = jnp.zeros((slots_all, width), jnp.bfloat16).at[slot].set(jnp.repeat(tokens, top, 0))
    send = send.reshape(experts, cap, width)
    arrived = lax.all_to_all(send, "expert", split_axis=0, concat_axis=0, tiled=True)
    packed = arrived.reshape(slots_all, width)
    result = expert_rows(
        packed,
        lax.all_gather(w_gate, "dp", axis=2, tiled=True)[0],
        lax.all_gather(w_up, "dp", axis=2, tiled=True)[0],
        lax.all_gather(w_down, "dp", axis=2, tiled=True)[0],
    )
    expert_out = result.astype(jnp.bfloat16)
    back = lax.all_to_all(
        expert_out.reshape(experts, cap, width), "expert", split_axis=0, concat_axis=0, tiled=True
    )
    picked = back.reshape(slots_all, width)[slot].reshape(tok_count, top, width)
    mixed = jnp.einsum("tk,tkd->td", router_weights, picked.astype(jnp.float32))
    return mixed.astype(jnp.bfloat16)


def dense_body(tokens, expert_ids, router_weights, w_gate, w_up, w_down):
    experts = lax.axis_size("expert")
    axes = ("expert", "dp") if lax.axis_size("dp") > 1 else "expert"
    chosen = expert_ids[:, :, None] == jnp.arange(experts, dtype=jnp.int32)[None, None, :]
    table = jnp.sum(jnp.where(chosen, router_weights[:, :, None], 0.0), 1)
    table = lax.all_gather(table, axes, axis=0, tiled=True)
    rows = lax.all_gather(tokens, axes, axis=0, tiled=True)
    mine = jnp.arange(experts, dtype=jnp.int32)[None, :] == lax.axis_index("expert")
    weight = jnp.sum(jnp.where(mine, table, 0.0), 1, keepdims=True)
    gate_val = jnp.dot(rows, w_gate[0], preferred_element_type=jnp.float32)
    up_val = jnp.dot(rows, w_up[0], preferred_element_type=jnp.float32)
    hidden = (jax.nn.silu(gate_val) * up_val).astype(jnp.bfloat16)
    out = lax.dot_general(
        hidden, w_down[0], (((1,), (1,)), ((), ())), preferred_element_type=jnp.float32
    )
    part = (out * weight).astype(jnp.bfloat16)
    return lax.psum_scatter(part, axes, scatter_dimension=0, tiled=True)


def body(tokens, expert_ids, router_weights, w_gate, w_up, w_down):
    tok_count, top = expert_ids.shape
    experts = lax.axis_size("expert")
    cap = max(2, min(tok_count, 2 * tok_count * top // experts))
    args = (tokens, expert_ids, router_weights, w_gate, w_up, w_down)
    if cap >= tok_count:
        return dense_body(*args)
    return routed_body(cap, *args)


def solution(mesh):
    in_specs = (
        P(("parts", "expert", "dp"), None),
        P(("parts", "expert", "dp"), None),
        P(("parts", "expert", "dp"), None),
        P("expert", None, "dp"),
        P("expert", None, "dp"),
        P("expert", None, "dp"),
    )
    out_specs = P(("parts", "expert", "dp"), None)
    return jax.shard_map(body, mesh=mesh, in_specs=in_specs, out_specs=out_specs, check_vma=False)
```

```python
import functools
import math

import jax
import jax.numpy as jnp
from jax import lax
from jax.experimental import pallas as pl
from jax.experimental.pallas import tpu as pltpu
from jax.sharding import PartitionSpec as P

LANES = 128
PARTS = 3


def expert_rows(rows, gate_w, up_w, down_w):
    total = rows.shape[0]
    block = math.gcd(total, 128)
    pieces = []
    for index in range(total // block):
        block_rows = rows[index * block : (index + 1) * block]
        gate_val = jnp.dot(block_rows, gate_w, preferred_element_type=jnp.float32)
        up_val = jnp.dot(block_rows, up_w, preferred_element_type=jnp.float32)
        hidden = (jax.nn.silu(gate_val) * up_val).astype(jnp.bfloat16)
        pieces.append(
            lax.dot_general(
                hidden, down_w, (((1,), (1,)), ((), ())), preferred_element_type=jnp.float32
            )
        )
    return jnp.concatenate(pieces, 0)


def routed_body(cap, tokens, expert_ids, router_weights, w_gate, w_up, w_down):
    tok_count, top = expert_ids.shape
    width = tokens.shape[1]
    experts = lax.axis_size("expert")
    slots_all = experts * cap
    flat_ids = expert_ids.reshape(-1)
    onehot = (flat_ids[:, None] == jnp.arange(experts, dtype=jnp.int32)[None, :]).astype(jnp.int32)
    before = jnp.cumsum(onehot, 0) - onehot
    position = jnp.sum(before * onehot, 1)
    slot = flat_ids * cap + position
    send = jnp.zeros((slots_all, width), jnp.bfloat16).at[slot].set(jnp.repeat(tokens, top, 0))
    send = send.reshape(experts, cap, width)
    arrived = lax.all_to_all(send, "expert", split_axis=0, concat_axis=0, tiled=True)
    packed = arrived.reshape(slots_all, width)
    result = expert_rows(
        packed,
        lax.all_gather(w_gate, "dp", axis=2, tiled=True)[0],
        lax.all_gather(w_up, "dp", axis=2, tiled=True)[0],
        lax.all_gather(w_down, "dp", axis=2, tiled=True)[0],
    )
    expert_out = result.astype(jnp.bfloat16)
    back = lax.all_to_all(
        expert_out.reshape(experts, cap, width), "expert", split_axis=0, concat_axis=0, tiled=True
    )
    picked = back.reshape(slots_all, width)[slot].reshape(tok_count, top, width)
    mixed = jnp.einsum("tk,tkd->td", router_weights, picked.astype(jnp.float32))
    return mixed.astype(jnp.bfloat16)


def dense_body(tokens, expert_ids, router_weights, w_gate, w_up, w_down):
    experts = lax.axis_size("expert")
    axes = ("expert", "dp") if lax.axis_size("dp") > 1 else "expert"
    chosen = expert_ids[:, :, None] == jnp.arange(experts, dtype=jnp.int32)[None, None, :]
    table = jnp.sum(jnp.where(chosen, router_weights[:, :, None], 0.0), 1)
    table = lax.all_gather(table, axes, axis=0, tiled=True)
    rows = lax.all_gather(tokens, axes, axis=0, tiled=True)
    mine = jnp.arange(experts, dtype=jnp.int32)[None, :] == lax.axis_index("expert")
    weight = jnp.sum(jnp.where(mine, table, 0.0), 1, keepdims=True)
    gate_val = jnp.dot(rows, w_gate[0], preferred_element_type=jnp.float32)
    up_val = jnp.dot(rows, w_up[0], preferred_element_type=jnp.float32)
    hidden = (jax.nn.silu(gate_val) * up_val).astype(jnp.bfloat16)
    out = lax.dot_general(
        hidden, w_down[0], (((1,), (1,)), ((), ())), preferred_element_type=jnp.float32
    )
    part = (out * weight).astype(jnp.bfloat16)
    return lax.psum_scatter(part, axes, scatter_dimension=0, tiled=True)


MESH = pl.DeviceIdType.MESH


def fused_kernel(
    depth,
    ext_ref, gate_hbm, up_hbm, down_hbm, out_ref,
    tok, gate_w, up_w, down_w, part, from_core, to_x, from_x, to_z, from_z,
    load_sem, own_sem,
    agz_send, agz_recv, agx_send, agx_recv, agc_send, agc_recv,
    rsc_send, rsc_recv, rsx_send, rsx_recv, rsz_send, rsz_recv,
):
    me = lax.axis_index("expert")
    core = lax.rem(me, 2)
    col = lax.rem(me // 2, 2)
    row = me // 4
    width = out_ref.shape[1]
    count = out_ref.shape[0]
    ff = gate_w.shape[1]

    def device(r, x, c):
        return {"expert": (r * 2 + x) * 2 + c}

    partner = device(row, col, 1 - core)
    beside = device(row, 1 - col, core)
    above = device(row + 1, col, core)
    below = device(row - 1, col, core)

    loads = [
        pltpu.make_async_copy(gate_hbm.at[0], gate_w, load_sem.at[0]),
        pltpu.make_async_copy(up_hbm.at[0], up_w, load_sem.at[1]),
        pltpu.make_async_copy(down_hbm.at[0], down_w, load_sem.at[2]),
    ]
    own = pltpu.make_async_copy(ext_ref, tok.at[row, core, col], own_sem.at[0])

    barrier = pltpu.get_barrier_semaphore()
    for other in (partner, beside):
        pl.semaphore_signal(barrier, inc=1, device_id=other, device_id_type=MESH)

    @pl.when(row > 0)
    def _():
        pl.semaphore_signal(barrier, inc=1, device_id=below, device_id_type=MESH)

    @pl.when(row < depth - 1)
    def _():
        pl.semaphore_signal(barrier, inc=1, device_id=above, device_id_type=MESH)

    own.start()
    for load in loads:
        load.start()
    pl.semaphore_wait(barrier, jnp.where((row > 0) & (row < depth - 1), 4, 3))

    def remote(src, dst, send_sem, recv_sem, target):
        return pltpu.make_async_remote_copy(
            src_ref=src, dst_ref=dst, send_sem=send_sem, recv_sem=recv_sem,
            device_id=target, device_id_type=MESH,
        )

    def gather_z(s, target, src=None):
        block = tok.at[s, core, col]
        way = 0 if target is above else 1
        return remote(block if src is None else src, block, agz_send.at[s, way], agz_recv.at[s], target)

    def gather_x(s, src=None):
        block = tok.at[s, core, col]
        return remote(block if src is None else src, block, agx_send.at[s], agx_recv.at[s], beside)

    def gather_c(s, x, which, src=None):
        block = tok.at[s, core, x]
        return remote(block if src is None else src, block, agc_send.at[s, which], agc_recv.at[s, which], partner)

    def reduce_c(s):
        return remote(part.at[s, 1 - core], from_core.at[s], rsc_send.at[s], rsc_recv.at[s], partner)

    def reduce_x(s):
        return remote(to_x.at[s], from_x.at[s], rsx_send.at[s], rsx_recv.at[s], beside)

    def reduce_z(s, target):
        way = 0 if target is above else 1
        return remote(to_z.at[s], from_z.at[way, s], rsz_send.at[s], rsz_recv.at[way, s], target)

    @pl.when(row < depth - 1)
    def _():
        gather_z(row, above, ext_ref).start()

    @pl.when(row > 0)
    def _():
        gather_z(row, below, ext_ref).start()

    gather_x(row, ext_ref).start()
    gather_c(row, col, 0, ext_ref).start()

    def arrive_z(dist):
        @pl.when(row - dist >= 0)
        def _():
            s = row - dist
            gather_z(s, above).wait_recv()

            @pl.when(row < depth - 1)
            def _():
                gather_z(s, above).start()

            gather_x(s).start()
            gather_c(s, col, 0).start()

        @pl.when(row + dist < depth)
        def _():
            s = row + dist
            gather_z(s, below).wait_recv()

            @pl.when(row > 0)
            def _():
                gather_z(s, below).start()

            gather_x(s).start()
            gather_c(s, col, 0).start()

    def slab(k):
        low = jnp.where(row + k < depth, row + k, depth - 1 - k)
        high = jnp.where(row - k >= 0, row - k, k)
        return jnp.where(row < depth // 2, low, high)

    lane = lax.broadcasted_iota(jnp.int32, (1, LANES), 1)
    pick = jnp.where((lane % (depth * 4) == me) & (lane < PARTS * depth * 4), 1.0, 0.0)
    block_cols = 512

    def compute(s):
        rows = tok[s].reshape(4 * count, width + LANES)
        weight = jnp.sum(rows[:, width:].astype(jnp.float32) * pick, 1, keepdims=True)
        rows = rows[:, :width]
        gate_val = jnp.dot(rows, gate_w[...], preferred_element_type=jnp.float32)
        up_val = jnp.dot(rows, up_w[...], preferred_element_type=jnp.float32)
        hidden = (gate_val / (1.0 + jnp.exp(-gate_val)) * up_val).astype(jnp.bfloat16)
        for at in range(0, width, block_cols):
            value = lax.dot_general(
                hidden, down_w[at : at + block_cols, :], (((1,), (1,)), ((), ())),
                preferred_element_type=jnp.float32,
            )
            part[s, :, :, :, at : at + block_cols] = (
                (value * weight).astype(jnp.bfloat16).reshape(2, 2, count, block_cols)
            )

    def reduce_over_core(s):
        reduce_c(s).wait_recv()
        total = part[s, core, 1 - col].astype(jnp.float32) + from_core[s, 1 - col].astype(jnp.float32)
        to_x[s] = total.astype(jnp.bfloat16)
        reduce_x(s).start()

    def column_sum(s):
        total = part[s, core, col].astype(jnp.float32) + from_core[s, col].astype(jnp.float32)
        return total + from_x[s].astype(jnp.float32)

    def send_z(s):
        reduce_x(s).wait_recv()

        def side(way, target, upstream):
            @pl.when(upstream)
            def _():
                reduce_z(s, target).wait_recv()
                total = column_sum(s) + from_z[way, s].astype(jnp.float32)
                to_z[s] = total.astype(jnp.bfloat16)

            @pl.when(jnp.logical_not(upstream))
            def _():
                to_z[s] = column_sum(s).astype(jnp.bfloat16)

            reduce_z(s, target).start()

        @pl.when(s > row)
        def _():
            side(0, above, row > 0)

        @pl.when(s < row)
        def _():
            side(1, below, row < depth - 1)

    own.wait()
    for k in range(depth):
        s = slab(k)
        if k + 1 < depth:
            arrive_z(k + 1)
        gather_x(s).wait_recv()
        gather_c(s, 1 - col, 1).start()
        gather_c(s, col, 0).wait_recv()
        gather_c(s, 1 - col, 1).wait_recv()
        if k == 0:
            for load in loads:
                load.wait()
        compute(s)
        reduce_c(s).start()
        if k >= 1:
            reduce_over_core(slab(k - 1))
    reduce_over_core(slab(depth - 1))
    for k in range(1, depth):
        send_z(slab(k))

    reduce_x(row).wait_recv()
    @pl.when(row < depth - 1)
    def _():
        reduce_z(row, below).wait_recv()

    @pl.when(row > 0)
    def _():
        reduce_z(row, above).wait_recv()

    @pl.when(row == 0)
    def _():
        out_ref[...] = (column_sum(row) + from_z[1, row].astype(jnp.float32)).astype(jnp.bfloat16)

    @pl.when(row == depth - 1)
    def _():
        out_ref[...] = (column_sum(row) + from_z[0, row].astype(jnp.float32)).astype(jnp.bfloat16)

    @pl.when((row > 0) & (row < depth - 1))
    def _():
        both = from_z[0, row].astype(jnp.float32) + from_z[1, row].astype(jnp.float32)
        out_ref[...] = (column_sum(row) + both).astype(jnp.bfloat16)

    for s in range(depth):
        gather_x(s).wait_send()
        gather_c(s, col, 0).wait_send()
        gather_c(s, col, 1).wait_send()
        reduce_c(s).wait_send()
        reduce_x(s).wait_send()

        @pl.when(row != s)
        def _():
            reduce_z(s, above).wait_send()

        @pl.when((row >= s) & (row < depth - 1))
        def _():
            gather_z(s, above).wait_send()

        @pl.when((row <= s) & (row > 0))
        def _():
            gather_z(s, below).wait_send()


def fused_body(tokens, expert_ids, router_weights, w_gate, w_up, w_down):
    experts = lax.axis_size("expert")
    depth = experts // 4
    count, width = tokens.shape
    ff = w_gate.shape[2]
    chosen = expert_ids[:, :, None] == jnp.arange(experts, dtype=jnp.int32)[None, None, :]
    left = jnp.sum(jnp.where(chosen, router_weights[:, :, None], 0.0), 1)
    terms = []
    for _ in range(PARTS):
        term = lax.reduce_precision(left, 8, 7)
        left = left - term
        terms.append(term.astype(jnp.bfloat16))
    pad = jnp.zeros((count, LANES - PARTS * experts), jnp.bfloat16)
    ext = jnp.concatenate([tokens] + terms + [pad], 1)
    wide = width + LANES
    bf16 = jnp.bfloat16
    dma = pltpu.SemaphoreType.DMA
    return pl.pallas_call(
        functools.partial(fused_kernel, depth),
        out_shape=jax.ShapeDtypeStruct((count, width), bf16),
        in_specs=[pl.BlockSpec(memory_space=pltpu.VMEM)] + [pl.BlockSpec(memory_space=pl.ANY)] * 3,
        out_specs=pl.BlockSpec(memory_space=pltpu.VMEM),
        scratch_shapes=[
            pltpu.VMEM((depth, 2, 2, count, wide), bf16),
            pltpu.VMEM((width, ff), bf16),
            pltpu.VMEM((width, ff), bf16),
            pltpu.VMEM((width, ff), bf16),
            pltpu.VMEM((depth, 2, 2, count, width), bf16),
            pltpu.VMEM((depth, 2, count, width), bf16),
            pltpu.VMEM((depth, count, width), bf16),
            pltpu.VMEM((depth, count, width), bf16),
            pltpu.VMEM((depth, count, width), bf16),
            pltpu.VMEM((2, depth, count, width), bf16),
            dma((3,)), dma((1,)),
            dma((depth, 2)), dma((depth,)), dma((depth,)), dma((depth,)), dma((depth, 2)), dma((depth, 2)),
            dma((depth,)), dma((depth,)), dma((depth,)), dma((depth,)), dma((depth,)), dma((2, depth)),
        ],
        compiler_params=pltpu.CompilerParams(
            collective_id=0, has_side_effects=True, vmem_limit_bytes=60 * 1024 * 1024
        ),
        name="moe",
    )(ext, w_gate, w_up, w_down)


def body(tokens, expert_ids, router_weights, w_gate, w_up, w_down):
    tok_count, top = expert_ids.shape
    experts = lax.axis_size("expert")
    cap = max(2, min(tok_count, 2 * tok_count * top // experts))
    args = (tokens, expert_ids, router_weights, w_gate, w_up, w_down)
    grid = experts % 4 == 0 and 8 <= experts <= 16 and lax.axis_size("dp") == 1
    if cap >= tok_count and grid:
        return fused_body(*args)
    if cap >= tok_count:
        return dense_body(*args)
    return routed_body(cap, *args)


def solution(mesh):
    in_specs = (
        P(("parts", "expert", "dp"), None),
        P(("parts", "expert", "dp"), None),
        P(("parts", "expert", "dp"), None),
        P("expert", None, "dp"),
        P("expert", None, "dp"),
        P("expert", None, "dp"),
    )
    out_specs = P(("parts", "expert", "dp"), None)
    return jax.shard_map(body, mesh=mesh, in_specs=in_specs, out_specs=out_specs, check_vma=False)
```

```python
import functools
import math

import jax
import jax.numpy as jnp
from jax import lax
from jax.experimental import pallas as pl
from jax.experimental.pallas import tpu as pltpu
from jax.sharding import PartitionSpec as P

LANES = 128
PARTS = 3


def expert_rows(rows, gate_w, up_w, down_w):
    total = rows.shape[0]
    block = math.gcd(total, 128)
    pieces = []
    for index in range(total // block):
        block_rows = rows[index * block : (index + 1) * block]
        gate_val = jnp.dot(block_rows, gate_w, preferred_element_type=jnp.float32)
        up_val = jnp.dot(block_rows, up_w, preferred_element_type=jnp.float32)
        hidden = (jax.nn.silu(gate_val) * up_val).astype(jnp.bfloat16)
        pieces.append(
            lax.dot_general(
                hidden, down_w, (((1,), (1,)), ((), ())), preferred_element_type=jnp.float32
            )
        )
    return jnp.concatenate(pieces, 0)


def routed_body(cap, tokens, expert_ids, router_weights, w_gate, w_up, w_down):
    tok_count, top = expert_ids.shape
    width = tokens.shape[1]
    experts = lax.axis_size("expert")
    slots_all = experts * cap
    flat_ids = expert_ids.reshape(-1)
    onehot = (flat_ids[:, None] == jnp.arange(experts, dtype=jnp.int32)[None, :]).astype(jnp.int32)
    before = jnp.cumsum(onehot, 0) - onehot
    position = jnp.sum(before * onehot, 1)
    slot = flat_ids * cap + position
    send = jnp.zeros((slots_all, width), jnp.bfloat16).at[slot].set(jnp.repeat(tokens, top, 0))
    send = send.reshape(experts, cap, width)
    arrived = lax.all_to_all(send, "expert", split_axis=0, concat_axis=0, tiled=True)
    packed = arrived.reshape(slots_all, width)
    result = expert_rows(
        packed,
        lax.all_gather(w_gate, "dp", axis=2, tiled=True)[0],
        lax.all_gather(w_up, "dp", axis=2, tiled=True)[0],
        lax.all_gather(w_down, "dp", axis=2, tiled=True)[0],
    )
    expert_out = result.astype(jnp.bfloat16)
    back = lax.all_to_all(
        expert_out.reshape(experts, cap, width), "expert", split_axis=0, concat_axis=0, tiled=True
    )
    picked = back.reshape(slots_all, width)[slot].reshape(tok_count, top, width)
    mixed = jnp.einsum("tk,tkd->td", router_weights, picked.astype(jnp.float32))
    return mixed.astype(jnp.bfloat16)


def dense_body(tokens, expert_ids, router_weights, w_gate, w_up, w_down):
    experts = lax.axis_size("expert")
    axes = ("expert", "dp") if lax.axis_size("dp") > 1 else "expert"
    chosen = expert_ids[:, :, None] == jnp.arange(experts, dtype=jnp.int32)[None, None, :]
    table = jnp.sum(jnp.where(chosen, router_weights[:, :, None], 0.0), 1)
    table = lax.all_gather(table, axes, axis=0, tiled=True)
    rows = lax.all_gather(tokens, axes, axis=0, tiled=True)
    mine = jnp.arange(experts, dtype=jnp.int32)[None, :] == lax.axis_index("expert")
    weight = jnp.sum(jnp.where(mine, table, 0.0), 1, keepdims=True)
    gate_val = jnp.dot(rows, w_gate[0], preferred_element_type=jnp.float32)
    up_val = jnp.dot(rows, w_up[0], preferred_element_type=jnp.float32)
    hidden = (jax.nn.silu(gate_val) * up_val).astype(jnp.bfloat16)
    out = lax.dot_general(
        hidden, w_down[0], (((1,), (1,)), ((), ())), preferred_element_type=jnp.float32
    )
    part = (out * weight).astype(jnp.bfloat16)
    return lax.psum_scatter(part, axes, scatter_dimension=0, tiled=True)


MESH = pl.DeviceIdType.MESH
CHUNKS = 4
X_FIRST = (0, 1, 2, 3)
Z_FIRST = ()


def fused_kernel(
    depth,
    ext_ref, gate_hbm, up_hbm, down_hbm, out_ref,
    tok, gate_w, up_w, down_w, part, from_core, to_x, from_x, to_z, from_z,
    load_sem, own_sem,
    agz_send, agz_recv, agx_send, agx_recv, agc_send, agc_recv,
    rsc_send, rsc_recv, rsx_send, rsx_recv, rsz_send, rsz_recv,
):
    me = lax.axis_index("expert")
    core = lax.rem(me, 2)
    col = lax.rem(me // 2, 2)
    row = me // 4
    width = out_ref.shape[1]
    count = out_ref.shape[0]
    ff = gate_w.shape[1]

    def device(r, x, c):
        return {"expert": (r * 2 + x) * 2 + c}

    partner = device(row, col, 1 - core)
    beside = device(row, 1 - col, core)
    above = device(row + 1, col, core)
    below = device(row - 1, col, core)

    loads = [
        pltpu.make_async_copy(gate_hbm.at[0], gate_w, load_sem.at[0]),
        pltpu.make_async_copy(up_hbm.at[0], up_w, load_sem.at[1]),
        pltpu.make_async_copy(down_hbm.at[0], down_w, load_sem.at[2]),
    ]
    own = pltpu.make_async_copy(ext_ref, tok.at[row, core, col], own_sem.at[0])

    barrier = pltpu.get_barrier_semaphore()
    for other in (partner, beside):
        pl.semaphore_signal(barrier, inc=1, device_id=other, device_id_type=MESH)

    @pl.when(row > 0)
    def _():
        pl.semaphore_signal(barrier, inc=1, device_id=below, device_id_type=MESH)

    @pl.when(row < depth - 1)
    def _():
        pl.semaphore_signal(barrier, inc=1, device_id=above, device_id_type=MESH)

    own.start()
    for load in loads:
        load.start()
    pl.semaphore_wait(barrier, jnp.where((row > 0) & (row < depth - 1), 4, 3))

    def remote(src, dst, send_sem, recv_sem, target):
        return pltpu.make_async_remote_copy(
            src_ref=src, dst_ref=dst, send_sem=send_sem, recv_sem=recv_sem,
            device_id=target, device_id_type=MESH,
        )

    def gather_z(s, target, src=None):
        block = tok.at[s, core, col]
        way = 0 if target is above else 1
        return remote(block if src is None else src, block, agz_send.at[s, way], agz_recv.at[s], target)

    def gather_x(s, src=None):
        block = tok.at[s, core, col]
        return remote(block if src is None else src, block, agx_send.at[s], agx_recv.at[s], beside)

    def gather_c(s, x, which, src=None):
        block = tok.at[s, core, x]
        return remote(block if src is None else src, block, agc_send.at[s, which], agc_recv.at[s, which], partner)

    def reduce_c(s):
        return remote(part.at[s, 1 - core], from_core.at[s], rsc_send.at[s], rsc_recv.at[s], partner)

    def reduce_x(s, q):
        return remote(to_x.at[s, q], from_x.at[s, q], rsx_send.at[s, q], rsx_recv.at[s, q], beside)

    def reduce_z(s, q, target):
        way = 0 if target is above else 1
        src, dst = to_z.at[s, q], from_z.at[way, s, q]
        if q in X_FIRST:
            src, dst = src.at[0], dst.at[0]
        return remote(src, dst, rsz_send.at[s, q], rsz_recv.at[way, s, q], target)

    @pl.when(row < depth - 1)
    def _():
        gather_z(row, above, ext_ref).start()

    @pl.when(row > 0)
    def _():
        gather_z(row, below, ext_ref).start()

    gather_x(row, ext_ref).start()
    gather_c(row, col, 0, ext_ref).start()

    def arrive_z(dist):
        @pl.when(row - dist >= 0)
        def _():
            s = row - dist
            gather_z(s, above).wait_recv()

            @pl.when(row < depth - 1)
            def _():
                gather_z(s, above).start()

            gather_x(s).start()
            gather_c(s, col, 0).start()

        @pl.when(row + dist < depth)
        def _():
            s = row + dist
            gather_z(s, below).wait_recv()

            @pl.when(row > 0)
            def _():
                gather_z(s, below).start()

            gather_x(s).start()
            gather_c(s, col, 0).start()

    def slab(k):
        low = jnp.where(row + k < depth, row + k, depth - 1 - k)
        high = jnp.where(row - k >= 0, row - k, k)
        return jnp.where(row < depth // 2, low, high)

    lane = lax.broadcasted_iota(jnp.int32, (1, LANES), 1)
    pick = jnp.where((lane % (depth * 4) == me) & (lane < PARTS * depth * 4), 1.0, 0.0)
    block_cols = 512

    def compute(s):
        rows = tok[s].reshape(4 * count, width + LANES)
        weight = jnp.sum(rows[:, width:].astype(jnp.float32) * pick, 1, keepdims=True)
        rows = rows[:, :width]
        gate_val = jnp.dot(rows, gate_w[...], preferred_element_type=jnp.float32)
        up_val = jnp.dot(rows, up_w[...], preferred_element_type=jnp.float32)
        hidden = (gate_val / (1.0 + jnp.exp(-gate_val)) * up_val).astype(jnp.bfloat16)
        for at in range(0, width, block_cols):
            value = lax.dot_general(
                hidden, down_w[at : at + block_cols, :], (((1,), (1,)), ((), ())),
                preferred_element_type=jnp.float32,
            )
            part[s, :, :, :, at : at + block_cols] = (
                (value * weight).astype(jnp.bfloat16).reshape(2, 2, count, block_cols)
            )

    cols = width // CHUNKS

    def core_sum(s, x, q):
        at = pl.ds(q * cols, cols)
        return part[s, core, x, :, at].astype(jnp.float32) + from_core[s, x, :, at].astype(jnp.float32)

    def column_sum(s, q):
        return core_sum(s, col, q) + from_x[s, q].astype(jnp.float32)

    def send_both(s, q, way, target, upstream):
        for x in range(2):
            total = core_sum(s, x, q)
            if upstream:
                total = total + from_z[way, s, q, x].astype(jnp.float32)
            to_z[s, q, x] = total.astype(jnp.bfloat16)
        reduce_z(s, q, target).start()

    def reduce_over_core(s):
        reduce_c(s).wait_recv()
        for q in X_FIRST:
            to_x[s, q] = core_sum(s, 1 - col, q).astype(jnp.bfloat16)
            reduce_x(s, q).start()

        @pl.when((s > row) & (row == 0))
        def _():
            for q in Z_FIRST:
                send_both(s, q, 0, above, False)

        @pl.when((s < row) & (row == depth - 1))
        def _():
            for q in Z_FIRST:
                send_both(s, q, 1, below, False)

    def send_early(s):
        def side(target):
            for q in X_FIRST:
                reduce_x(s, q).wait_recv()
                to_z[s, q, 0] = column_sum(s, q).astype(jnp.bfloat16)
                reduce_z(s, q, target).start()

        @pl.when((s > row) & (row == 0))
        def _():
            side(above)

        @pl.when((s < row) & (row == depth - 1))
        def _():
            side(below)

    def send_z(s):
        def side(way, target, upstream):
            @pl.when(upstream)
            def _():
                for q in Z_FIRST:
                    reduce_z(s, q, target).wait_recv()
                    send_both(s, q, way, target, True)
                for q in X_FIRST:
                    reduce_x(s, q).wait_recv()
                    reduce_z(s, q, target).wait_recv()
                    total = column_sum(s, q) + from_z[way, s, q, 0].astype(jnp.float32)
                    to_z[s, q, 0] = total.astype(jnp.bfloat16)
                    reduce_z(s, q, target).start()

        @pl.when(s > row)
        def _():
            side(0, above, row > 0)

        @pl.when(s < row)
        def _():
            side(1, below, row < depth - 1)

    def finish(ways):
        def arrived(q, x):
            total = from_z[ways[0], row, q, x].astype(jnp.float32)
            for way in ways[1:]:
                total = total + from_z[way, row, q, x].astype(jnp.float32)
            return total

        for q in Z_FIRST + X_FIRST:
            for way in ways:
                reduce_z(row, q, above if way == 0 else below).wait_recv()
            at = pl.ds(q * cols, cols)
            if q in Z_FIRST:
                total = core_sum(row, 1 - col, q) + arrived(q, 1 - col)
                to_x[row, q] = total.astype(jnp.bfloat16)
                reduce_x(row, q).start()
            else:
                reduce_x(row, q).wait_recv()
                out_ref[:, at] = (column_sum(row, q) + arrived(q, 0)).astype(jnp.bfloat16)
        for q in Z_FIRST:
            at = pl.ds(q * cols, cols)
            reduce_x(row, q).wait_recv()
            out_ref[:, at] = (column_sum(row, q) + arrived(q, col)).astype(jnp.bfloat16)

    own.wait()
    for k in range(depth):
        s = slab(k)
        if k + 1 < depth:
            arrive_z(k + 1)
        gather_x(s).wait_recv()
        gather_c(s, 1 - col, 1).start()
        gather_c(s, col, 0).wait_recv()
        gather_c(s, 1 - col, 1).wait_recv()
        if k == 0:
            for load in loads:
                load.wait()
        compute(s)
        reduce_c(s).start()
        if k >= 2:
            reduce_over_core(slab(k - 1))
        if k >= 3:
            send_early(slab(k - 2))
    reduce_over_core(slab(depth - 1))
    reduce_over_core(row)
    for k in range(1, depth):
        if k >= depth - 2:
            send_early(slab(k))
        send_z(slab(k))

    @pl.when(row == 0)
    def _():
        finish((1,))

    @pl.when(row == depth - 1)
    def _():
        finish((0,))

    @pl.when((row > 0) & (row < depth - 1))
    def _():
        finish((0, 1))

    for s in range(depth):
        gather_x(s).wait_send()
        gather_c(s, col, 0).wait_send()
        gather_c(s, col, 1).wait_send()
        reduce_c(s).wait_send()
        for q in X_FIRST:
            reduce_x(s, q).wait_send()

        @pl.when(row == s)
        def _():
            for q in Z_FIRST:
                reduce_x(s, q).wait_send()

        @pl.when(row != s)
        def _():
            for q in range(CHUNKS):
                reduce_z(s, q, above).wait_send()

        @pl.when((row >= s) & (row < depth - 1))
        def _():
            gather_z(s, above).wait_send()

        @pl.when((row <= s) & (row > 0))
        def _():
            gather_z(s, below).wait_send()


def fused_body(tokens, expert_ids, router_weights, w_gate, w_up, w_down):
    experts = lax.axis_size("expert")
    depth = experts // 4
    count, width = tokens.shape
    ff = w_gate.shape[2]
    chosen = expert_ids[:, :, None] == jnp.arange(experts, dtype=jnp.int32)[None, None, :]
    left = jnp.sum(jnp.where(chosen, router_weights[:, :, None], 0.0), 1)
    terms = []
    for _ in range(PARTS):
        term = lax.reduce_precision(left, 8, 7)
        left = left - term
        terms.append(term.astype(jnp.bfloat16))
    pad = jnp.zeros((count, LANES - PARTS * experts), jnp.bfloat16)
    ext = jnp.concatenate([tokens] + terms + [pad], 1)
    wide = width + LANES
    bf16 = jnp.bfloat16
    dma = pltpu.SemaphoreType.DMA
    return pl.pallas_call(
        functools.partial(fused_kernel, depth),
        out_shape=jax.ShapeDtypeStruct((count, width), bf16),
        in_specs=[pl.BlockSpec(memory_space=pltpu.VMEM)] + [pl.BlockSpec(memory_space=pl.ANY)] * 3,
        out_specs=pl.BlockSpec(memory_space=pltpu.VMEM),
        scratch_shapes=[
            pltpu.VMEM((depth, 2, 2, count, wide), bf16),
            pltpu.VMEM((width, ff), bf16),
            pltpu.VMEM((width, ff), bf16),
            pltpu.VMEM((width, ff), bf16),
            pltpu.VMEM((depth, 2, 2, count, width), bf16),
            pltpu.VMEM((depth, 2, count, width), bf16),
            pltpu.VMEM((depth, CHUNKS, count, width // CHUNKS), bf16),
            pltpu.VMEM((depth, CHUNKS, count, width // CHUNKS), bf16),
            pltpu.VMEM((depth, CHUNKS, 2, count, width // CHUNKS), bf16),
            pltpu.VMEM((2, depth, CHUNKS, 2, count, width // CHUNKS), bf16),
            dma((3,)), dma((1,)),
            dma((depth, 2)), dma((depth,)), dma((depth,)), dma((depth,)), dma((depth, 2)), dma((depth, 2)),
            dma((depth,)), dma((depth,)), dma((depth, CHUNKS)), dma((depth, CHUNKS)), dma((depth, CHUNKS)), dma((2, depth, CHUNKS)),
        ],
        compiler_params=pltpu.CompilerParams(
            collective_id=0, has_side_effects=True, vmem_limit_bytes=60 * 1024 * 1024
        ),
        name="moe",
    )(ext, w_gate, w_up, w_down)


def body(tokens, expert_ids, router_weights, w_gate, w_up, w_down):
    tok_count, top = expert_ids.shape
    experts = lax.axis_size("expert")
    cap = max(2, min(tok_count, 2 * tok_count * top // experts))
    args = (tokens, expert_ids, router_weights, w_gate, w_up, w_down)
    grid = experts % 4 == 0 and 8 <= experts <= 16 and lax.axis_size("dp") == 1
    if cap >= tok_count and grid:
        return fused_body(*args)
    if cap >= tok_count:
        return dense_body(*args)
    return routed_body(cap, *args)


def solution(mesh):
    in_specs = (
        P(("parts", "expert", "dp"), None),
        P(("parts", "expert", "dp"), None),
        P(("parts", "expert", "dp"), None),
        P("expert", None, "dp"),
        P("expert", None, "dp"),
        P("expert", None, "dp"),
    )
    out_specs = P(("parts", "expert", "dp"), None)
    return jax.shard_map(body, mesh=mesh, in_specs=in_specs, out_specs=out_specs, check_vma=False)
```

```python
import functools
import math

import jax
import jax.numpy as jnp
from jax import lax
from jax.experimental import pallas as pl
from jax.experimental.pallas import tpu as pltpu
from jax.sharding import PartitionSpec as P

LANES = 128
PARTS = 3


def expert_rows(rows, gate_w, up_w, down_w):
    total = rows.shape[0]
    block = math.gcd(total, 128)
    pieces = []
    for index in range(total // block):
        block_rows = rows[index * block : (index + 1) * block]
        gate_val = jnp.dot(block_rows, gate_w, preferred_element_type=jnp.float32)
        up_val = jnp.dot(block_rows, up_w, preferred_element_type=jnp.float32)
        hidden = (jax.nn.silu(gate_val) * up_val).astype(jnp.bfloat16)
        pieces.append(
            lax.dot_general(
                hidden, down_w, (((1,), (1,)), ((), ())), preferred_element_type=jnp.float32
            )
        )
    return jnp.concatenate(pieces, 0)


def routed_body(cap, tokens, expert_ids, router_weights, w_gate, w_up, w_down):
    tok_count, top = expert_ids.shape
    width = tokens.shape[1]
    experts = lax.axis_size("expert")
    slots_all = experts * cap
    flat_ids = expert_ids.reshape(-1)
    onehot = (flat_ids[:, None] == jnp.arange(experts, dtype=jnp.int32)[None, :]).astype(jnp.int32)
    before = jnp.cumsum(onehot, 0) - onehot
    position = jnp.sum(before * onehot, 1)
    slot = flat_ids * cap + position
    send = jnp.zeros((slots_all, width), jnp.bfloat16).at[slot].set(jnp.repeat(tokens, top, 0))
    send = send.reshape(experts, cap, width)
    arrived = lax.all_to_all(send, "expert", split_axis=0, concat_axis=0, tiled=True)
    packed = arrived.reshape(slots_all, width)
    result = expert_rows(
        packed,
        lax.all_gather(w_gate, "dp", axis=2, tiled=True)[0],
        lax.all_gather(w_up, "dp", axis=2, tiled=True)[0],
        lax.all_gather(w_down, "dp", axis=2, tiled=True)[0],
    )
    expert_out = result.astype(jnp.bfloat16)
    back = lax.all_to_all(
        expert_out.reshape(experts, cap, width), "expert", split_axis=0, concat_axis=0, tiled=True
    )
    picked = back.reshape(slots_all, width)[slot].reshape(tok_count, top, width)
    mixed = jnp.einsum("tk,tkd->td", router_weights, picked.astype(jnp.float32))
    return mixed.astype(jnp.bfloat16)


def dense_body(tokens, expert_ids, router_weights, w_gate, w_up, w_down):
    experts = lax.axis_size("expert")
    axes = ("expert", "dp") if lax.axis_size("dp") > 1 else "expert"
    chosen = expert_ids[:, :, None] == jnp.arange(experts, dtype=jnp.int32)[None, None, :]
    table = jnp.sum(jnp.where(chosen, router_weights[:, :, None], 0.0), 1)
    table = lax.all_gather(table, axes, axis=0, tiled=True)
    rows = lax.all_gather(tokens, axes, axis=0, tiled=True)
    mine = jnp.arange(experts, dtype=jnp.int32)[None, :] == lax.axis_index("expert")
    weight = jnp.sum(jnp.where(mine, table, 0.0), 1, keepdims=True)
    gate_val = jnp.dot(rows, w_gate[0], preferred_element_type=jnp.float32)
    up_val = jnp.dot(rows, w_up[0], preferred_element_type=jnp.float32)
    hidden = (jax.nn.silu(gate_val) * up_val).astype(jnp.bfloat16)
    out = lax.dot_general(
        hidden, w_down[0], (((1,), (1,)), ((), ())), preferred_element_type=jnp.float32
    )
    part = (out * weight).astype(jnp.bfloat16)
    return lax.psum_scatter(part, axes, scatter_dimension=0, tiled=True)


MESH = pl.DeviceIdType.MESH
CHUNKS = 4
X_FIRST = (0, 1, 2, 3)
Z_FIRST = ()


def fused_kernel(
    depth,
    token_ref, table_ref, gate_hbm, up_hbm, down_hbm, out_ref,
    tok, gate_w, up_w, down_w, part, from_core, to_x, from_x, to_z, from_z,
    load_sem, own_sem,
    agz_send, agz_recv, agx_send, agx_recv, agc_send, agc_recv,
    rsc_send, rsc_recv, rsx_send, rsx_recv, rsz_send, rsz_recv,
):
    me = lax.axis_index("expert")
    core = lax.rem(me, 2)
    col = lax.rem(me // 2, 2)
    row = me // 4
    width = out_ref.shape[1]
    count = out_ref.shape[0]
    ff = gate_w.shape[1]

    def device(r, x, c):
        return {"expert": (r * 2 + x) * 2 + c}

    partner = device(row, col, 1 - core)
    beside = device(row, 1 - col, core)
    above = device(row + 1, col, core)
    below = device(row - 1, col, core)

    loads = [
        pltpu.make_async_copy(gate_hbm.at[0], gate_w, load_sem.at[0]),
        pltpu.make_async_copy(up_hbm.at[0], up_w, load_sem.at[1]),
        pltpu.make_async_copy(down_hbm.at[0], down_w, load_sem.at[2]),
    ]
    owns = [
        pltpu.make_async_copy(
            token_ref, tok.at[row, core, col, :, pl.ds(0, width)], own_sem.at[0]
        ),
        pltpu.make_async_copy(
            table_ref, tok.at[row, core, col, :, pl.ds(width, LANES)], own_sem.at[1]
        ),
    ]

    barrier = pltpu.get_barrier_semaphore()
    for other in (partner, beside):
        pl.semaphore_signal(barrier, inc=1, device_id=other, device_id_type=MESH)

    @pl.when(row > 0)
    def _():
        pl.semaphore_signal(barrier, inc=1, device_id=below, device_id_type=MESH)

    @pl.when(row < depth - 1)
    def _():
        pl.semaphore_signal(barrier, inc=1, device_id=above, device_id_type=MESH)

    for own in owns:
        own.start()
    for load in loads:
        load.start()
    pl.semaphore_wait(barrier, jnp.where((row > 0) & (row < depth - 1), 4, 3))

    def remote(src, dst, send_sem, recv_sem, target):
        return pltpu.make_async_remote_copy(
            src_ref=src, dst_ref=dst, send_sem=send_sem, recv_sem=recv_sem,
            device_id=target, device_id_type=MESH,
        )

    def gather_z(s, target, src=None):
        block = tok.at[s, core, col]
        way = 0 if target is above else 1
        return remote(block if src is None else src, block, agz_send.at[s, way], agz_recv.at[s], target)

    def gather_x(s, src=None):
        block = tok.at[s, core, col]
        return remote(block if src is None else src, block, agx_send.at[s], agx_recv.at[s], beside)

    def gather_c(s, x, which, src=None):
        block = tok.at[s, core, x]
        return remote(block if src is None else src, block, agc_send.at[s, which], agc_recv.at[s, which], partner)

    def reduce_c(s):
        return remote(part.at[s, 1 - core], from_core.at[s], rsc_send.at[s], rsc_recv.at[s], partner)

    def reduce_x(s, q):
        return remote(to_x.at[s, q], from_x.at[s, q], rsx_send.at[s, q], rsx_recv.at[s, q], beside)

    def reduce_z(s, q, target):
        way = 0 if target is above else 1
        src, dst = to_z.at[s, q], from_z.at[way, s, q]
        if q in X_FIRST:
            src, dst = src.at[0], dst.at[0]
        return remote(src, dst, rsz_send.at[s, q], rsz_recv.at[way, s, q], target)

    for own in owns:
        own.wait()

    @pl.when(row < depth - 1)
    def _():
        gather_z(row, above).start()

    @pl.when(row > 0)
    def _():
        gather_z(row, below).start()

    gather_x(row).start()
    gather_c(row, col, 0).start()

    def arrive_z(dist):
        @pl.when(row - dist >= 0)
        def _():
            s = row - dist
            gather_z(s, above).wait_recv()

            @pl.when(row < depth - 1)
            def _():
                gather_z(s, above).start()

            gather_x(s).start()
            gather_c(s, col, 0).start()

        @pl.when(row + dist < depth)
        def _():
            s = row + dist
            gather_z(s, below).wait_recv()

            @pl.when(row > 0)
            def _():
                gather_z(s, below).start()

            gather_x(s).start()
            gather_c(s, col, 0).start()

    def slab(k):
        low = jnp.where(row + k < depth, row + k, depth - 1 - k)
        high = jnp.where(row - k >= 0, row - k, k)
        return jnp.where(row < depth // 2, low, high)

    lane = lax.broadcasted_iota(jnp.int32, (1, LANES), 1)
    pick = jnp.where((lane % (depth * 4) == me) & (lane < PARTS * depth * 4), 1.0, 0.0)
    block_cols = 512

    def compute(s):
        rows = tok[s].reshape(4 * count, width + LANES)
        weight = jnp.sum(rows[:, width:].astype(jnp.float32) * pick, 1, keepdims=True)
        rows = rows[:, :width]
        gate_val = jnp.dot(rows, gate_w[...], preferred_element_type=jnp.float32)
        up_val = jnp.dot(rows, up_w[...], preferred_element_type=jnp.float32)
        hidden = (gate_val / (1.0 + jnp.exp(-gate_val)) * up_val).astype(jnp.bfloat16)
        for at in range(0, width, block_cols):
            value = lax.dot_general(
                hidden, down_w[at : at + block_cols, :], (((1,), (1,)), ((), ())),
                preferred_element_type=jnp.float32,
            )
            part[s, :, :, :, at : at + block_cols] = (
                (value * weight).astype(jnp.bfloat16).reshape(2, 2, count, block_cols)
            )

    cols = width // CHUNKS

    def core_sum(s, x, q):
        at = pl.ds(q * cols, cols)
        return part[s, core, x, :, at].astype(jnp.float32) + from_core[s, x, :, at].astype(jnp.float32)

    def column_sum(s, q):
        return core_sum(s, col, q) + from_x[s, q].astype(jnp.float32)

    def send_both(s, q, way, target, upstream):
        for x in range(2):
            total = core_sum(s, x, q)
            if upstream:
                total = total + from_z[way, s, q, x].astype(jnp.float32)
            to_z[s, q, x] = total.astype(jnp.bfloat16)
        reduce_z(s, q, target).start()

    def reduce_over_core(s):
        reduce_c(s).wait_recv()
        for q in X_FIRST:
            to_x[s, q] = core_sum(s, 1 - col, q).astype(jnp.bfloat16)
            reduce_x(s, q).start()

        @pl.when((s > row) & (row == 0))
        def _():
            for q in Z_FIRST:
                send_both(s, q, 0, above, False)

        @pl.when((s < row) & (row == depth - 1))
        def _():
            for q in Z_FIRST:
                send_both(s, q, 1, below, False)

    def send_early(s):
        def side(target):
            for q in X_FIRST:
                reduce_x(s, q).wait_recv()
                to_z[s, q, 0] = column_sum(s, q).astype(jnp.bfloat16)
                reduce_z(s, q, target).start()

        @pl.when((s > row) & (row == 0))
        def _():
            side(above)

        @pl.when((s < row) & (row == depth - 1))
        def _():
            side(below)

    def send_z(s):
        def side(way, target, upstream):
            @pl.when(upstream)
            def _():
                for q in Z_FIRST:
                    reduce_z(s, q, target).wait_recv()
                    send_both(s, q, way, target, True)
                for q in X_FIRST:
                    reduce_x(s, q).wait_recv()
                    reduce_z(s, q, target).wait_recv()
                    total = column_sum(s, q) + from_z[way, s, q, 0].astype(jnp.float32)
                    to_z[s, q, 0] = total.astype(jnp.bfloat16)
                    reduce_z(s, q, target).start()

        @pl.when(s > row)
        def _():
            side(0, above, row > 0)

        @pl.when(s < row)
        def _():
            side(1, below, row < depth - 1)

    def finish(ways):
        def arrived(q, x):
            total = from_z[ways[0], row, q, x].astype(jnp.float32)
            for way in ways[1:]:
                total = total + from_z[way, row, q, x].astype(jnp.float32)
            return total

        for q in Z_FIRST + X_FIRST:
            for way in ways:
                reduce_z(row, q, above if way == 0 else below).wait_recv()
            at = pl.ds(q * cols, cols)
            if q in Z_FIRST:
                total = core_sum(row, 1 - col, q) + arrived(q, 1 - col)
                to_x[row, q] = total.astype(jnp.bfloat16)
                reduce_x(row, q).start()
            else:
                reduce_x(row, q).wait_recv()
                out_ref[:, at] = (column_sum(row, q) + arrived(q, 0)).astype(jnp.bfloat16)
        for q in Z_FIRST:
            at = pl.ds(q * cols, cols)
            reduce_x(row, q).wait_recv()
            out_ref[:, at] = (column_sum(row, q) + arrived(q, col)).astype(jnp.bfloat16)

    for k in range(depth):
        s = slab(k)
        if k + 1 < depth:
            arrive_z(k + 1)
        gather_x(s).wait_recv()
        gather_c(s, 1 - col, 1).start()
        gather_c(s, col, 0).wait_recv()
        gather_c(s, 1 - col, 1).wait_recv()
        if k == 0:
            for load in loads:
                load.wait()
        compute(s)
        reduce_c(s).start()
        if k >= 2:
            reduce_over_core(slab(k - 1))
        if k >= 3:
            send_early(slab(k - 2))
    reduce_over_core(slab(depth - 1))
    reduce_over_core(row)
    for k in range(1, depth):
        if k >= depth - 2:
            send_early(slab(k))
        send_z(slab(k))

    @pl.when(row == 0)
    def _():
        finish((1,))

    @pl.when(row == depth - 1)
    def _():
        finish((0,))

    @pl.when((row > 0) & (row < depth - 1))
    def _():
        finish((0, 1))

    for s in range(depth):
        gather_x(s).wait_send()
        gather_c(s, col, 0).wait_send()
        gather_c(s, col, 1).wait_send()
        reduce_c(s).wait_send()
        for q in X_FIRST:
            reduce_x(s, q).wait_send()

        @pl.when(row == s)
        def _():
            for q in Z_FIRST:
                reduce_x(s, q).wait_send()

        @pl.when(row != s)
        def _():
            for q in range(CHUNKS):
                reduce_z(s, q, above).wait_send()

        @pl.when((row >= s) & (row < depth - 1))
        def _():
            gather_z(s, above).wait_send()

        @pl.when((row <= s) & (row > 0))
        def _():
            gather_z(s, below).wait_send()


def fused_body(tokens, expert_ids, router_weights, w_gate, w_up, w_down):
    experts = lax.axis_size("expert")
    depth = experts // 4
    count, width = tokens.shape
    ff = w_gate.shape[2]
    chosen = expert_ids[:, :, None] == jnp.arange(experts, dtype=jnp.int32)[None, None, :]
    left = jnp.sum(jnp.where(chosen, router_weights[:, :, None], 0.0), 1)
    terms = []
    for _ in range(PARTS):
        term = lax.reduce_precision(left, 8, 7)
        left = left - term
        terms.append(term.astype(jnp.bfloat16))
    pad = jnp.zeros((count, LANES - PARTS * experts), jnp.bfloat16)
    table = jnp.concatenate(terms + [pad], 1)
    wide = width + LANES
    bf16 = jnp.bfloat16
    dma = pltpu.SemaphoreType.DMA
    return pl.pallas_call(
        functools.partial(fused_kernel, depth),
        out_shape=jax.ShapeDtypeStruct((count, width), bf16),
        in_specs=[pl.BlockSpec(memory_space=pl.ANY)] * 5,
        out_specs=pl.BlockSpec(memory_space=pltpu.VMEM),
        scratch_shapes=[
            pltpu.VMEM((depth, 2, 2, count, wide), bf16),
            pltpu.VMEM((width, ff), bf16),
            pltpu.VMEM((width, ff), bf16),
            pltpu.VMEM((width, ff), bf16),
            pltpu.VMEM((depth, 2, 2, count, width), bf16),
            pltpu.VMEM((depth, 2, count, width), bf16),
            pltpu.VMEM((depth, CHUNKS, count, width // CHUNKS), bf16),
            pltpu.VMEM((depth, CHUNKS, count, width // CHUNKS), bf16),
            pltpu.VMEM((depth, CHUNKS, 2, count, width // CHUNKS), bf16),
            pltpu.VMEM((2, depth, CHUNKS, 2, count, width // CHUNKS), bf16),
            dma((3,)), dma((2,)),
            dma((depth, 2)), dma((depth,)), dma((depth,)), dma((depth,)), dma((depth, 2)), dma((depth, 2)),
            dma((depth,)), dma((depth,)), dma((depth, CHUNKS)), dma((depth, CHUNKS)), dma((depth, CHUNKS)), dma((2, depth, CHUNKS)),
        ],
        compiler_params=pltpu.CompilerParams(
            collective_id=0, has_side_effects=True, vmem_limit_bytes=60 * 1024 * 1024
        ),
        name="moe",
    )(tokens, table, w_gate, w_up, w_down)


def body(tokens, expert_ids, router_weights, w_gate, w_up, w_down):
    tok_count, top = expert_ids.shape
    experts = lax.axis_size("expert")
    cap = max(2, min(tok_count, 2 * tok_count * top // experts))
    args = (tokens, expert_ids, router_weights, w_gate, w_up, w_down)
    grid = experts % 4 == 0 and 8 <= experts <= 16 and lax.axis_size("dp") == 1
    if cap >= tok_count and grid:
        return fused_body(*args)
    if cap >= tok_count:
        return dense_body(*args)
    return routed_body(cap, *args)


def solution(mesh):
    in_specs = (
        P(("parts", "expert", "dp"), None),
        P(("parts", "expert", "dp"), None),
        P(("parts", "expert", "dp"), None),
        P("expert", None, "dp"),
        P("expert", None, "dp"),
        P("expert", None, "dp"),
    )
    out_specs = P(("parts", "expert", "dp"), None)
    return jax.shard_map(body, mesh=mesh, in_specs=in_specs, out_specs=out_specs, check_vma=False)
```
